32 devices in a mesh: member: 2 (over x), blk: 8 (over z, y), feat: 2 (over core).
Axes of the slice: x: 2, y: 2, z: 4, core: 2. Of those that a mesh axis runs over, the one named last changes fastest.
Arguments:
- features: bfloat16 [256, 4096], P(('member', 'feat'), 'blk'), parts along dimension 0, may hold values from -6 to 6
- w_node: bfloat16 [4, 128, 128], P('member', None, 'feat'), parts along dimension 0, may hold values from -0.5 to 0.5
- w_msg: bfloat16 [4, 128, 128], P('member', None, 'feat'), parts along dimension 0, may hold values from -1.5 to 1.5
- w_mix: bfloat16 [4, 128, 128], P('member', 'feat'), parts along dimension 0, may hold values from -0.5 to 0.5
- hbias: float32 [4, 128], P('member', 'feat'), parts along dimension 0, may hold values from -3 to 3
- obias: float32 [4, 128], P('member', 'feat'), parts along dimension 0, may hold values from -3 to 3
- anchor_node: bfloat16 [4, 128, 128], P('member', None, 'feat'), parts along dimension 0, may hold values from -0.5 to 0.5
- anchor_msg: bfloat16 [4, 128, 128], P('member', None, 'feat'), parts along dimension 0, may hold values from -1.5 to 1.5
- anchor_mix: bfloat16 [4, 128, 128], P('member', 'feat'), parts along dimension 0, may hold values from -0.5 to 0.5
- cotangent: bfloat16 [256, 4096], P(('member', 'feat'), 'blk'), parts along dimension 0, may hold values from -0.09375 to 0.09375
- tile_cols: int32 [64, 12], P(('member', 'blk')), parts along dimension 0, may hold values from 0 to 31, as said below
- tile_count: int32 [64], P(('member', 'blk')), parts along dimension 0, may hold values from 3 to 12, as said below
- tile_masks: int32 [64, 12, 128, 128], P(('member', 'blk')), parts along dimension 0, may hold values 0 or 1
Outputs:
- out_features: bfloat16 [256, 4096], P(('member', 'feat'), 'blk'), parts along dimension 0
- grad_node: float32 [4, 128, 128], P('member', None, 'feat'), parts along dimension 0
- grad_msg: float32 [4, 128, 128], P('member', None, 'feat'), parts along dimension 0
- grad_mix: float32 [4, 128, 128], P('member', 'feat'), parts along dimension 0
- grad_hbias: float32 [4, 128], P('member', 'feat'), parts along dimension 0
- grad_obias: float32 [4, 128], P('member', 'feat'), parts along dimension 0
The draws below stay inside these ranges and needn't reach their ends.
There are 2 independent parts, one for each index of `member`. The reference program is written for one: setup_inputs(seed, part) draws one part's arguments, and reference() takes and returns one part's arrays. A program takes and returns all parts, laid end to end along the dimension named above; each array names one. Nothing has to cross between parts.
Inputs may be any that keep to these rules, and one draw needn't show every extreme that they name: Only slots 0 to tile_count[r] - 1 of block row r are used; some block row has exactly 12 live slots. Slot 0 of every block row names the row's own block. For every slot of row r, the blk index holding the named block (tile_cols // 4) lies within 1 step of r // 4 around the closed cycle of 8 indices; slot 1 lies exactly 1 step ahead and slot 2 exactly 1 step behind in every row.
All inputs are finite; a program needn't handle non-finite values. No bound on the sum of `tile_masks` on one device may be relied on, other than what follows from the above.
Results may differ from the reference program's by a relative error of at most 0.01.
Values may be sent and summed in bfloat16 or wider, within the bound.
A program may use at most 64 MiB of HBM per device.

```python
import jax
import jax.numpy as jnp
from jax import lax

F = 128
HID = 128
TILE = 128
KMAX = 12
LAYERS = 2
BR_DEV = 4
NBLK = 32
NODES = 4096
REACH = 1


def tile_layout(key):
    key = jax.random.fold_in(key, 11)
    key_count, key_top, key_offset, key_within = jax.random.split(key, 4)
    counts = jax.random.randint(key_count, (NBLK,), 3, KMAX + 1, dtype=jnp.int32)
    fullest = jax.random.randint(key_top, (), 0, NBLK, dtype=jnp.int32)
    blocks = jnp.arange(NBLK, dtype=jnp.int32)
    counts = jnp.where(blocks == fullest, KMAX, counts).astype(jnp.int32)
    offsets = jax.random.randint(key_offset, (NBLK, KMAX), -REACH, REACH + 1, dtype=jnp.int32)
    offsets = offsets.at[:, 0].set(0).at[:, 1].set(REACH).at[:, 2].set(-REACH)
    within = jax.random.randint(key_within, (NBLK, KMAX), 0, BR_DEV, dtype=jnp.int32)
    within = within.at[:, 0].set(blocks % BR_DEV)
    owner = blocks // BR_DEV
    cycle_size = NBLK // BR_DEV
    columns = (owner[:, None] + offsets) % cycle_size * BR_DEV + within
    return (counts, columns.astype(jnp.int32))


def draw_tile_cols(key, part):
    return tile_layout(key)[1]


def draw_tile_count(key, part):
    return tile_layout(key)[0]


def plant(drawn, key, low, high):
    shape = drawn.shape
    spot = [jax.random.randint(jax.random.fold_in(key, axis), (), 0, shape[axis]) for axis in range(len(shape))]
    drawn = drawn.at[tuple(spot)].set(low)
    longest = shape.index(max(shape))
    spot[longest] = (spot[longest] + 1) % shape[longest]
    return drawn.at[tuple(spot)].set(high)


def levels(stream_key, dims, shards, smallest, high):
    gain = 1.0
    for dim, blocks in shards:
        steps = jax.random.uniform(jax.random.fold_in(jax.random.fold_in(stream_key, 6), dim), (blocks,), jnp.float32, smallest / len(shards), high / len(shards))
        gain = gain * jnp.repeat(jnp.exp(steps), dims[dim] // blocks).reshape((-1,) + (1,) * (len(dims) - 1 - dim))
    return gain


def scatter_about(stream_key, extent, scale, reach, shards=(), kind=jnp.bfloat16):
    drawn = scale * jax.random.normal(stream_key, extent, jnp.float32)
    if shards:
        drawn = drawn * levels(stream_key, extent, shards, -0.22, 0.18)
    return jnp.clip(drawn, -reach, reach).astype(kind)


def setup_inputs(seed: int = 0, part: int = 0) -> dict:
    seeds = jax.random.split(jax.random.key(seed), 14)
    part_keys = jax.random.split(jax.random.fold_in(seeds[13], part), 14)
    features = scatter_about(part_keys[0], (F, NODES), 1.0, 6.0, ((0, 2), (1, 8)))
    w_node = scatter_about(part_keys[1], (LAYERS, F, HID), F ** -0.5, 0.5, ((2, 2),))
    w_msg = scatter_about(part_keys[2], (LAYERS, F, HID), (F // 8) ** -0.5, 1.5, ((2, 2),))
    w_mix = scatter_about(part_keys[3], (LAYERS, HID, F), HID ** -0.5, 0.5, ((1, 2),))
    hbias = scatter_about(part_keys[4], (LAYERS, HID), 0.5, 3.0, ((1, 2),), jnp.float32)
    obias = scatter_about(part_keys[5], (LAYERS, F), 0.5, 3.0, ((1, 2),), jnp.float32)
    anchor_node = scatter_about(part_keys[6], (LAYERS, F, HID), F ** -0.5, 0.5, ((2, 2),))
    anchor_msg = scatter_about(part_keys[7], (LAYERS, F, HID), (F // 8) ** -0.5, 1.5, ((2, 2),))
    anchor_mix = scatter_about(part_keys[8], (LAYERS, HID, F), HID ** -0.5, 0.5, ((1, 2),))
    cotangent = scatter_about(part_keys[9], (F, NODES), (1.0 / NODES ** 0.5), 0.09375, ((0, 2), (1, 8)))
    tile_cols = draw_tile_cols(jax.random.fold_in(jax.random.fold_in(seeds[13], part), 71), part)
    tile_count = draw_tile_count(jax.random.fold_in(jax.random.fold_in(seeds[13], part), 71), part)
    tile_masks = plant((jax.random.randint(part_keys[12], (NBLK, KMAX, TILE, TILE), 0, 32) < 1).astype(jnp.int32), jax.random.fold_in(part_keys[12], 1), 0, 1)
    return {"features": features, "w_node": w_node, "w_msg": w_msg, "w_mix": w_mix, "hbias": hbias, "obias": obias, "anchor_node": anchor_node, "anchor_msg": anchor_msg, "anchor_mix": anchor_mix, "cotangent": cotangent, "tile_cols": tile_cols, "tile_count": tile_count, "tile_masks": tile_masks}


def apply_live(tile_count, tile_masks):
    live_flags = (jnp.arange(KMAX, dtype=jnp.int32)[None, :] < tile_count[:, None]).astype(jnp.int32)
    return tile_masks * live_flags[:, :, None, None]


def aggregate(acts, tile_cols, live_masks):
    blocks = acts.reshape(F, NBLK, TILE)

    def one_row(pair):
        column_ids, masks = pair
        chosen = jnp.take(blocks, column_ids, axis=1).astype(jnp.float32)
        return jnp.einsum('fkj,kij->fi', chosen, masks.astype(jnp.float32))

    per_row = lax.map(one_row, (tile_cols, live_masks))
    return jnp.transpose(per_row, (1, 0, 2)).reshape(F, NODES)


def spread(share, tile_cols, live_masks):
    blocks = share.reshape(F, NBLK, TILE).astype(jnp.float32)

    def one_row(total, triple):
        row_index, column_ids, masks = triple
        source = lax.dynamic_index_in_dim(blocks, row_index, 1, keepdims=False)
        parts = jnp.einsum('fi,kij->kfj', source, masks.astype(jnp.float32))
        return total.at[column_ids].add(parts), None

    total, unused = lax.scan(one_row, jnp.zeros((NBLK, F, TILE), jnp.float32),
                             (jnp.arange(NBLK, dtype=jnp.int32), tile_cols, live_masks))
    return jnp.transpose(total, (1, 0, 2)).reshape(F, NODES)


def matmul(left, right):
    return jnp.dot(left, right, preferred_element_type=jnp.float32)


def reference(features, w_node, w_msg, w_mix, hbias, obias, anchor_node, anchor_msg, anchor_mix, cotangent, tile_cols, tile_count, tile_masks):
    live_masks = apply_live(tile_count, tile_masks)
    degree = (1 + jnp.sum(live_masks, axis=(1, 3))).astype(jnp.float32).reshape(NODES)
    acts = features
    saved = []
    for layer in range(LAYERS):
        summed = aggregate(acts, tile_cols, live_masks)
        message = ((acts.astype(jnp.float32) + summed) / degree[None, :]).astype(jnp.bfloat16)
        pre = matmul(w_node[layer].T, acts) + matmul(w_msg[layer].T, message) + hbias[layer][:, None]
        hidden = jax.nn.silu(pre).astype(jnp.bfloat16)
        output = (acts.astype(jnp.float32) + matmul(w_mix[layer].T, hidden) + obias[layer][:, None]).astype(jnp.bfloat16)
        saved.append((acts, message, pre, hidden))
        acts = output
    grads_node = [None] * LAYERS
    grads_msg = [None] * LAYERS
    grads_mix = [None] * LAYERS
    grads_hbias = [None] * LAYERS
    grads_obias = [None] * LAYERS
    d_out = cotangent
    for layer in range(LAYERS - 1, -1, -1):
        inputs, message, pre, hidden = saved[layer]
        grads_obias[layer] = jnp.sum(d_out.astype(jnp.float32), axis=1)
        d_hidden = matmul(w_mix[layer], d_out)
        sigma = jax.nn.sigmoid(pre)
        d_pre = d_hidden * sigma * (1.0 + pre * (1.0 - sigma))
        grads_hbias[layer] = jnp.sum(d_pre, axis=1)
        d_round = d_pre.astype(jnp.bfloat16)
        grads_node[layer] = matmul(inputs, d_round.T) + (w_node[layer].astype(jnp.float32) - anchor_node[layer].astype(jnp.float32))
        grads_msg[layer] = matmul(message, d_round.T) + (w_msg[layer].astype(jnp.float32) - anchor_msg[layer].astype(jnp.float32))
        grads_mix[layer] = matmul(hidden, d_out.T) + (w_mix[layer].astype(jnp.float32) - anchor_mix[layer].astype(jnp.float32))
        if layer > 0:
            d_in = matmul(w_node[layer], d_round)
            d_message = matmul(w_msg[layer], d_round)
            share = (d_message / degree[None, :]).astype(jnp.bfloat16)
            back = spread(share, tile_cols, live_masks)
            d_out = (d_out.astype(jnp.float32) + d_in + share.astype(jnp.float32) + back).astype(jnp.bfloat16)
    return (acts, jnp.stack(grads_node), jnp.stack(grads_msg), jnp.stack(grads_mix),
            jnp.stack(grads_hbias), jnp.stack(grads_obias))
```

```python
import functools

import jax
import jax.numpy as jnp
from jax import lax
from jax.experimental import pallas as pl
from jax.experimental.pallas import tpu as pltpu
from jax.sharding import PartitionSpec as P

F32 = jnp.float32
BF16 = jnp.bfloat16
MESH = pl.DeviceIdType.MESH


def mm(left, right):
    return jnp.dot(left, right, preferred_element_type=F32)


def mm_nt(left, right):
    return lax.dot_general(left, right, (((1,), (1,)), ((), ())), preferred_element_type=F32)


def eye(size):
    rows = lax.broadcasted_iota(jnp.int32, (size, size), 0)
    cols = lax.broadcasted_iota(jnp.int32, (size, size), 1)
    return rows == cols


def to_column(row):
    size = row.shape[1]
    return jnp.sum(jnp.where(eye(size), jnp.broadcast_to(row, (size, size)), 0.0), axis=1, keepdims=True)


def to_row(column):
    size = column.shape[0]
    return jnp.sum(jnp.where(eye(size), jnp.broadcast_to(column, (size, size)), 0.0), axis=0, keepdims=True)


def kernel(
    n, reach, layers, br, slots, tile, half, nodes,
    cols, count, feats, w_node, w_msg, w_mix, hbias, obias, a_node, a_msg, a_mix, cot, masks,
    out_x, g_node, g_msg, g_mix, g_hb, g_ob,
    mask_v, mask_b, adj, xwin, xm, wt, wmix, wmixt, wback, bias, dy, pre_s, hid, dr, dh, part_out, part_in,
    gbuf, grecv, gred,
    s_mask, s_xs, s_xr, s_ps, s_pr, s_fs, s_fr, s_gs, s_gr, s_as, s_ar,
):
    feat = 2 * half
    me = lax.axis_index("blk")
    side = lax.axis_index("feat")
    peer = 1 - side
    wins = 2 * reach + 1
    own = pl.ds(pl.multiple_of(side * half, half), half)
    own_msg = pl.ds(pl.multiple_of(feat + side * half, half), half)
    far = pl.ds(pl.multiple_of(peer * half, half), half)
    chunk = gbuf.shape[2]

    def at(step):
        return lax.rem(me + step + n, n)

    barrier = pltpu.get_barrier_semaphore()
    pl.semaphore_signal(barrier, inc=1, device_id={"feat": peer}, device_id_type=MESH)
    for step in range(1, n):
        pl.semaphore_signal(barrier, inc=1, device_id={"blk": at(step)}, device_id_type=MESH)

    mask_copies = [pltpu.make_async_copy(masks.at[r], mask_v.at[r], s_mask.at[r]) for r in range(br)]
    for copy in mask_copies:
        copy.start()

    xm[0, own] = feats[...]
    xwin[0, reach] = feats[...]
    dy[layers - 1, own] = cot[...]
    unit = jnp.where(eye(half), 1.0, 0.0).astype(BF16)
    for l in range(layers):
        wt[l, own, 0:feat] = mm_nt(unit, w_node[l]).astype(BF16)
        wt[l, own, feat : 2 * feat] = mm_nt(unit, w_msg[l]).astype(BF16)
        wmix[l, own] = w_mix[l]
    bias[side] = jnp.zeros(bias.shape[1:], F32)
    bias[side, 0:layers, 0:half] = hbias[...]
    bias[side, layers : 2 * layers, 0:half] = obias[...]

    pl.semaphore_wait(barrier, n)

    pending = []

    def send(src, dst, s_send, s_recv, device):
        copy = pltpu.make_async_remote_copy(
            src_ref=src, dst_ref=dst, send_sem=s_send, recv_sem=s_recv, device_id=device, device_id_type=MESH
        )
        copy.start()
        pending.append(copy)
        return copy

    def spread_out(src, l):
        copies = []
        for step in range(1, reach + 1):
            for sign in (1, -1):
                slot = reach - sign * step
                copies.append(
                    (slot, send(src, xwin.at[l, slot], s_xs.at[l, slot], s_xr.at[l, slot], {"blk": at(sign * step)}))
                )
        return copies

    def to_peer(index, src, dst):
        return send(src, dst, s_fs.at[index], s_fr.at[index], {"feat": peer})

    arriving = spread_out(feats, 0)
    first = [
        to_peer(0, wmix.at[:, own], wmix.at[:, own]),
        to_peer(1, wt.at[:, own], wt.at[:, own]),
        to_peer(2, bias.at[side], bias.at[side]),
        to_peer(3, dy.at[layers - 1, own], dy.at[layers - 1, own]),
        to_peer(4, xm.at[0, own], xm.at[0, own]),
    ]

    for r in range(br):
        mask_copies[r].wait()

    def build_row(r, unused):
        for k in range(slots):
            mask_b[k] = mask_v[r, k].astype(F32).astype(BF16)
        live = count[r]
        targets = []
        for k in range(slots):
            name = cols[r, k]
            block = lax.rem(lax.div(name, br) - me + reach + n, n) * br + lax.rem(name, br)
            targets.append(jnp.where(k < live, block, -1))

        def build_dev(j, unused):
            rows = pl.ds(pl.multiple_of(r * tile, tile), tile)
            for c in range(br):
                total = jnp.zeros((tile, tile), BF16)
                for k in range(slots):
                    hit = jnp.where(targets[k] == j * br + c, 1.0, 0.0).astype(F32)
                    total = total + jnp.full((tile, tile), hit, F32).astype(BF16) * mask_b[k]
                adj[j, rows, c * tile : (c + 1) * tile] = total
            return unused

        return lax.fori_loop(0, wins, build_dev, unused)

    lax.fori_loop(0, br, build_row, 0)
    ones = jnp.ones((16, nodes), BF16)
    degree = mm_nt(ones, adj[0])
    for j in range(1, wins):
        degree = degree + mm_nt(ones, adj[j])
    inverse = 1.0 / (degree[0:1] + 1.0)

    for copy in first[0:4]:
        copy.wait_recv()
    unit_f = jnp.where(eye(feat), 1.0, 0.0).astype(BF16)
    hb, ob = [], []
    for l in range(layers):
        wmixt[l] = mm_nt(unit_f, wmix[l]).astype(BF16)
        if l > 0:
            wback[l, 0:feat] = mm_nt(unit_f, wt[l, :, 0:feat]).astype(BF16)
            wback[l, feat : 2 * feat] = mm_nt(unit_f, wt[l, :, feat : 2 * feat]).astype(BF16)
        hb.append(
            jnp.concatenate([to_column(bias[s, l : l + 1, 0:half]) for s in range(2)], axis=0)
        )
        ob.append([to_column(bias[s, layers + l : layers + l + 1, 0:half]) for s in (side, peer)])
    dh[...] = mm(wmix[layers - 1], dy[layers - 1])
    first[4].wait_recv()

    for l in range(layers):
        summed = mm_nt(xwin[l, reach], adj[reach])
        for slot, copy in arriving:
            copy.wait_recv()
            summed = summed + mm_nt(xwin[l, slot], adj[slot])
        message = (xm[l, own].astype(F32) + summed) * inverse
        xm[l, own_msg] = message.astype(BF16)
        copy = to_peer(5 + l, xm.at[l, own_msg], xm.at[l, own_msg])
        part = mm(wt[l, :, 0:feat], xm[l, 0:feat]) + hb[l]
        copy.wait_recv()
        pre = part + mm(wt[l, :, feat : 2 * feat], xm[l, feat : 2 * feat])
        sigma = 1.0 / (1.0 + jnp.exp(-pre))
        hidden = (pre * sigma).astype(BF16)
        hid[l] = hidden
        slope = sigma * (1.0 + pre * (1.0 - sigma))
        pre_s[l] = slope
        if l + 1 < layers:
            after = (xm[l, own].astype(F32) + mm(wmixt[l, own], hidden) + ob[l][0]).astype(BF16)
            xm[l + 1, own] = after
            xwin[l + 1, reach] = after
            arriving = spread_out(xwin.at[l + 1, reach], l + 1)
            xm[l + 1, far] = (xm[l, far].astype(F32) + mm(wmixt[l, far], hidden) + ob[l][1]).astype(BF16)

    def reduce_start(l):
        copies = []
        for step in range(1, n):
            to = at(step)
            copies.append(
                send(gbuf.at[l, to], grecv.at[l, step - 1], s_gs.at[l, step - 1], s_gr.at[l, step - 1], {"blk": to})
            )
        return copies

    def reduce_end(l, copies):
        total = gbuf[l, me]
        for step in range(1, n):
            copies[step - 1].wait_recv()
            total = total + grecv[l, step - 1]
        gred[l, me] = total
        return [
            send(gred.at[l, me], gred.at[l, me], s_as.at[l, step - 1], s_ar.at[l, step - 1], {"blk": at(step)})
            for step in range(1, n)
        ]

    def finish(l, copies):
        for copy in copies:
            copy.wait_recv()
        per = feat // chunk
        both = gred[l, 0:per].reshape(feat, 2 * half)
        g_node[l] = both[:, 0:half] + (w_node[l].astype(F32) - a_node[l].astype(F32))
        g_msg[l] = both[:, half : 2 * half] + (w_msg[l].astype(F32) - a_msg[l].astype(F32))
        more = half // chunk
        mixed = gred[l, per : per + more].reshape(half, feat)
        g_mix[l] = mixed + (w_mix[l].astype(F32) - a_mix[l].astype(F32))
        g_hb[l : l + 1] = gred[l, per + more, 0:1, 0:half]
        g_ob[l : l + 1] = gred[l, per + more, 1:2, 0:half]

    def gradients(l, d_own, d_round_own, dy_own):
        zero = jnp.zeros((half, nodes), BF16)
        both = mm_nt(xm[l, 0:feat], jnp.concatenate([d_round_own, zero], axis=0)) + mm_nt(
            xm[l, feat : 2 * feat], jnp.concatenate([zero, d_round_own], axis=0)
        )
        per = feat // chunk
        more = half // chunk
        gbuf[l, 0:per] = both.reshape(per, chunk, 2 * half)
        gbuf[l, per : per + more] = mm_nt(hid[l, own], dy[l]).reshape(more, chunk, feat)
        gbuf[l, per + more :] = jnp.zeros((n - per - more, chunk, 2 * half), F32)
        gbuf[l, per + more, 0:1, 0:half] = to_row(jnp.sum(d_own, axis=1, keepdims=True))
        gbuf[l, per + more, 1:2, 0:half] = to_row(jnp.sum(dy_own, axis=1, keepdims=True))

    reducing = {}
    for l in range(layers - 1, -1, -1):
        dy_own = dy[l, own].astype(F32)
        if l > 0:
            if l < layers - 1:
                dh[...] = mm(wmix[l], dy[l])
            d_pre = dh[...] * pre_s[l]
            d_round = d_pre.astype(BF16)
            dr[...] = d_round
            dh[...] = d_pre
            share = (mm(wback[l, own_msg], d_round) * inverse).astype(BF16)
            incoming = []
            for step in range(1, reach + 1):
                for sign in (1, -1):
                    slot = reach + sign * step
                    part_out[l - 1, slot] = mm(share, adj[slot]).astype(BF16)
                    landing = reach - sign * step
                    incoming.append(
                        (
                            landing,
                            send(
                                part_out.at[l - 1, slot],
                                part_in.at[l - 1, landing],
                                s_ps.at[l - 1, landing],
                                s_pr.at[l - 1, landing],
                                {"blk": at(sign * step)},
                            ),
                        )
                    )
            before = dy_own + mm(wback[l, own], d_round) + share.astype(F32) + mm(share, adj[reach])
            if l == layers - 1:
                last = xm[l, own].astype(F32) + mm(wmixt[l, own], hid[l]) + ob[l][0]
                out_x[...] = last.astype(BF16)
            gradients(l, dh[own], dr[own], dy_own)
            reducing[l] = reduce_start(l)
            for landing, copy in incoming:
                copy.wait_recv()
                before = before + part_in[l - 1, landing].astype(F32)
            dy[l - 1, own] = before.astype(BF16)
            copy = to_peer(5 + layers + l, dy.at[l - 1, own], dy.at[l - 1, own])
            copy.wait_recv()
        else:
            d_own = mm(wmix[l, own], dy[l]) * pre_s[l, own]
            gradients(l, d_own, d_own.astype(BF16), dy_own)
            reducing[l] = reduce_start(l)
    sharing = {}
    for l in range(layers - 1, -1, -1):
        sharing[l] = reduce_end(l, reducing[l])
    for l in range(layers - 1, -1, -1):
        finish(l, sharing[l])
    for copy in pending:
        copy.wait_send()


def local(
    features, w_node, w_msg, w_mix, hbias, obias, anchor_node, anchor_msg, anchor_mix, cotangent,
    tile_cols, tile_count, tile_masks,
):
    br, slots, tile, _ = tile_masks.shape
    half, nodes = features.shape
    feat = 2 * half
    layers = w_node.shape[0]
    n = lax.axis_size("blk")
    reach = max(1, n // 8)
    wins = 2 * reach + 1
    chunk = max(8, 256 // n)
    dma = pltpu.SemaphoreType.DMA
    vmem = pl.BlockSpec(memory_space=pltpu.VMEM)
    smem = pl.BlockSpec(memory_space=pltpu.SMEM)
    return pl.pallas_call(
        functools.partial(kernel, n, reach, layers, br, slots, tile, half, nodes),
        out_shape=(
            jax.ShapeDtypeStruct((half, nodes), BF16),
            jax.ShapeDtypeStruct((layers, feat, half), F32),
            jax.ShapeDtypeStruct((layers, feat, half), F32),
            jax.ShapeDtypeStruct((layers, half, feat), F32),
            jax.ShapeDtypeStruct((layers, half), F32),
            jax.ShapeDtypeStruct((layers, half), F32),
        ),
        in_specs=[smem, smem] + [vmem] * 10 + [pl.BlockSpec(memory_space=pl.ANY)],
        out_specs=(vmem,) * 6,
        scratch_shapes=[
            pltpu.VMEM((br, slots, tile, tile), jnp.int32),
            pltpu.VMEM((slots, tile, tile), BF16),
            pltpu.VMEM((wins, nodes, nodes), BF16),
            pltpu.VMEM((layers, wins, half, nodes), BF16),
            pltpu.VMEM((layers, 2 * feat, nodes), BF16),
            pltpu.VMEM((layers, feat, 2 * feat), BF16),
            pltpu.VMEM((layers, feat, feat), BF16),
            pltpu.VMEM((layers, feat, feat), BF16),
            pltpu.VMEM((layers, 2 * feat, feat), BF16),
            pltpu.VMEM((2, 8, 128), F32),
            pltpu.VMEM((layers, feat, nodes), BF16),
            pltpu.VMEM((layers, feat, nodes), F32),
            pltpu.VMEM((layers, feat, nodes), BF16),
            pltpu.VMEM((feat, nodes), BF16),
            pltpu.VMEM((feat, nodes), F32),
            pltpu.VMEM((layers - 1, wins, half, nodes), BF16),
            pltpu.VMEM((layers - 1, wins, half, nodes), BF16),
            pltpu.VMEM((layers, n, chunk, feat), F32),
            pltpu.VMEM((layers, n - 1, chunk, feat), F32),
            pltpu.VMEM((layers, n, chunk, feat), F32),
            dma((br,)),
            dma((layers, wins)),
            dma((layers, wins)),
            dma((layers - 1, wins)),
            dma((layers - 1, wins)),
            dma((5 + 2 * layers + 1,)),
            dma((5 + 2 * layers + 1,)),
            dma((layers, n - 1)),
            dma((layers, n - 1)),
            dma((layers, n - 1)),
            dma((layers, n - 1)),
        ],
        compiler_params=pltpu.CompilerParams(
            collective_id=0, has_side_effects=True, vmem_limit_bytes=50 * 1024 * 1024
        ),
        name="graph_net",
    )(
        tile_cols, tile_count, features, w_node, w_msg, w_mix, hbias, obias,
        anchor_node, anchor_msg, anchor_mix, cotangent, tile_masks,
    )


def solution(mesh):
    placed = (
        P(("member", "feat"), "blk"),
        P("member", None, "feat"),
        P("member", None, "feat"),
        P("member", "feat", None),
        P("member", "feat"),
        P("member", "feat"),
        P("member", None, "feat"),
        P("member", None, "feat"),
        P("member", "feat", None),
        P(("member", "feat"), "blk"),
        P(("member", "blk"), None),
        P(("member", "blk")),
        P(("member", "blk"), None, None, None),
    )
    return jax.shard_map(
        local,
        mesh=mesh,
        in_specs=placed,
        out_specs=(
            P(("member", "feat"), "blk"),
            P("member", None, "feat"),
            P("member", None, "feat"),
            P("member", "feat", None),
            P("member", "feat"),
            P("member", "feat"),
        ),
        check_vma=False,
    )
```

```python
import functools

import jax
import jax.numpy as jnp
from jax import lax
from jax.experimental import pallas as pl
from jax.experimental.pallas import tpu as pltpu
from jax.sharding import PartitionSpec as P

F32 = jnp.float32
BF16 = jnp.bfloat16
MESH = pl.DeviceIdType.MESH


def mm(left, right):
    return jnp.dot(left, right, preferred_element_type=F32)


def mm_nt(left, right):
    return lax.dot_general(left, right, (((1,), (1,)), ((), ())), preferred_element_type=F32)


def eye(size):
    rows = lax.broadcasted_iota(jnp.int32, (size, size), 0)
    cols = lax.broadcasted_iota(jnp.int32, (size, size), 1)
    return rows == cols


def to_column(row):
    size = row.shape[1]
    return jnp.sum(jnp.where(eye(size), jnp.broadcast_to(row, (size, size)), 0.0), axis=1, keepdims=True)


def to_row(column):
    size = column.shape[0]
    return jnp.sum(jnp.where(eye(size), jnp.broadcast_to(column, (size, size)), 0.0), axis=0, keepdims=True)


def kernel(
    n, reach, layers, br, slots, tile, half, nodes,
    cols, count, feats, w_node, w_msg, w_mix, hbias, obias, cot, masks,
    out_x, gred,
    cols_s, count_s, hb_v, ob_v, mask_v, mask_b, adj, xwin, xm, wt, wmix, wmixt, wback, bias, dy, pre_s, hid, dr, dh, part_out, part_in,
    gbuf, grecv,
    s_in, s_mask, s_xs, s_xr, s_ps, s_pr, s_fs, s_fr, s_gs, s_gr, s_as, s_ar,
):
    feat = 2 * half
    me = lax.axis_index("blk")
    side = lax.axis_index("feat")
    peer = 1 - side
    wins = 2 * reach + 1
    own = pl.ds(pl.multiple_of(side * half, half), half)
    own_msg = pl.ds(pl.multiple_of(feat + side * half, half), half)
    far = pl.ds(pl.multiple_of(peer * half, half), half)
    chunk = gbuf.shape[2]

    def at(step):
        return lax.rem(me + step + n, n)

    barrier = pltpu.get_barrier_semaphore()
    pl.semaphore_signal(barrier, inc=1, device_id={"feat": peer}, device_id_type=MESH)
    for step in range(1, n):
        pl.semaphore_signal(barrier, inc=1, device_id={"blk": at(step)}, device_id_type=MESH)

    moves = [
        (cols, cols_s),
        (count, count_s),
        (hbias, hb_v),
        (obias, ob_v),
        (feats, xm.at[0, own]),
        (feats, xwin.at[0, reach]),
        (cot, dy.at[layers - 1, own]),
        (w_node, wt.at[:, own, 0:feat]),
        (w_msg, wt.at[:, own, feat : 2 * feat]),
        (w_mix, wmix.at[:, own]),
    ]
    loads = [pltpu.make_async_copy(src, dst, s_in.at[i]) for i, (src, dst) in enumerate(moves)]
    for copy in loads[0:4]:
        copy.start()
    mask_copies = [pltpu.make_async_copy(masks.at[r], mask_v.at[r], s_mask.at[r]) for r in range(br)]
    for copy in loads[4:] + mask_copies:
        copy.start()
    for copy in loads[0:4]:
        copy.wait()
    bias[side] = jnp.zeros(bias.shape[1:], F32)
    bias[side, 0:layers, 0:half] = hb_v[...]
    bias[side, layers : 2 * layers, 0:half] = ob_v[...]

    pl.semaphore_wait(barrier, n)

    pending = []

    def send(src, dst, s_send, s_recv, device):
        copy = pltpu.make_async_remote_copy(
            src_ref=src, dst_ref=dst, send_sem=s_send, recv_sem=s_recv, device_id=device, device_id_type=MESH
        )
        copy.start()
        pending.append(copy)
        return copy

    def spread_out(src, l):
        copies = []
        for step in range(1, reach + 1):
            for sign in (1, -1):
                slot = reach - sign * step
                copies.append(
                    (slot, send(src, xwin.at[l, slot], s_xs.at[l, slot], s_xr.at[l, slot], {"blk": at(sign * step)}))
                )
        return copies

    def to_peer(index, src, dst):
        return send(src, dst, s_fs.at[index], s_fr.at[index], {"feat": peer})

    arriving = spread_out(feats, 0)
    first = [
        to_peer(0, w_mix, wmix.at[:, own]),
        to_peer(1, w_node, wt.at[:, own, 0:feat]),
        to_peer(2, w_msg, wt.at[:, own, feat : 2 * feat]),
        to_peer(3, bias.at[side], bias.at[side]),
        to_peer(4, cot, dy.at[layers - 1, own]),
        to_peer(5, feats, xm.at[0, own]),
    ]

    for r in range(br):
        mask_copies[r].wait()

    def build_row(r, unused):
        for k in range(slots):
            mask_b[k] = mask_v[r, k].astype(F32).astype(BF16)
        live = count_s[r]
        targets = []
        for k in range(slots):
            name = cols_s[r, k]
            block = lax.rem(lax.div(name, br) - me + reach + n, n) * br + lax.rem(name, br)
            targets.append(jnp.where(k < live, block, -1))

        def build_dev(j, unused):
            rows = pl.ds(pl.multiple_of(r * tile, tile), tile)
            for c in range(br):
                total = jnp.zeros((tile, tile), BF16)
                for k in range(slots):
                    hit = jnp.where(targets[k] == j * br + c, 1.0, 0.0).astype(F32)
                    total = total + jnp.full((tile, tile), hit, F32).astype(BF16) * mask_b[k]
                adj[j, rows, c * tile : (c + 1) * tile] = total
            return unused

        return lax.fori_loop(0, wins, build_dev, unused)

    lax.fori_loop(0, br, build_row, 0)
    ones = jnp.ones((16, nodes), BF16)
    degree = mm_nt(ones, adj[0])
    for j in range(1, wins):
        degree = degree + mm_nt(ones, adj[j])
    inverse = 1.0 / (degree[0:1] + 1.0)

    for copy in loads[4:]:
        copy.wait()
    for copy in first[0:5]:
        copy.wait_recv()
    unit_f = jnp.where(eye(feat), 1.0, 0.0).astype(BF16)
    hb, ob = [], []
    for l in range(layers):
        wmixt[l] = mm_nt(unit_f, wmix[l]).astype(BF16)
        if l > 0:
            wback[l, 0:feat] = mm_nt(unit_f, wt[l, :, 0:feat]).astype(BF16)
            wback[l, feat : 2 * feat] = mm_nt(unit_f, wt[l, :, feat : 2 * feat]).astype(BF16)
        hb.append(
            jnp.concatenate([to_column(bias[s, l : l + 1, 0:half]) for s in range(2)], axis=0)
        )
        ob.append([to_column(bias[s, layers + l : layers + l + 1, 0:half]) for s in (side, peer)])
    dh[...] = mm(wmix[layers - 1], dy[layers - 1])
    first[5].wait_recv()

    for l in range(layers):
        summed = mm_nt(xwin[l, reach], adj[reach])
        for slot, copy in arriving:
            copy.wait_recv()
            summed = summed + mm_nt(xwin[l, slot], adj[slot])
        message = (xm[l, own].astype(F32) + summed) * inverse
        xm[l, own_msg] = message.astype(BF16)
        copy = to_peer(6 + l, xm.at[l, own_msg], xm.at[l, own_msg])
        part = mm(wt[l, :, 0:feat], xm[l, 0:feat]) + hb[l]
        copy.wait_recv()
        pre = part + mm(wt[l, :, feat : 2 * feat], xm[l, feat : 2 * feat])
        sigma = 1.0 / (1.0 + jnp.exp(-pre))
        hidden = (pre * sigma).astype(BF16)
        hid[l] = hidden
        slope = sigma * (1.0 + pre * (1.0 - sigma))
        pre_s[l] = slope
        if l + 1 < layers:
            after = (xm[l, own].astype(F32) + mm(wmixt[l, own], hidden) + ob[l][0]).astype(BF16)
            xm[l + 1, own] = after
            xwin[l + 1, reach] = after
            arriving = spread_out(xwin.at[l + 1, reach], l + 1)
            xm[l + 1, far] = (xm[l, far].astype(F32) + mm(wmixt[l, far], hidden) + ob[l][1]).astype(BF16)

    def reduce_start(l):
        copies = []
        for step in range(1, n):
            to = at(step)
            copies.append(
                send(gbuf.at[l, to], grecv.at[l, step - 1], s_gs.at[l, step - 1], s_gr.at[l, step - 1], {"blk": to})
            )
        return copies

    def reduce_end(l, copies):
        total = gbuf[l, me]
        for step in range(1, n):
            copies[step - 1].wait_recv()
            total = total + grecv[l, step - 1]
        gred[l, me] = total
        return [
            send(gred.at[l, me], gred.at[l, me], s_as.at[l, step - 1], s_ar.at[l, step - 1], {"blk": at(step)})
            for step in range(1, n)
        ]

    def gradients(l, d_own, d_round_own, dy_own):
        per = half // chunk
        gbuf[l, 0:per] = mm_nt(d_round_own, xm[l, 0:feat]).reshape(per, chunk, feat)
        gbuf[l, per : 2 * per] = mm_nt(d_round_own, xm[l, feat : 2 * feat]).reshape(per, chunk, feat)
        gbuf[l, 2 * per : 3 * per] = mm_nt(hid[l, own], dy[l]).reshape(per, chunk, feat)
        gbuf[l, 3 * per :] = jnp.zeros((n - 3 * per, chunk, feat), F32)
        gbuf[l, 3 * per, 0:1, 0:half] = to_row(jnp.sum(d_own, axis=1, keepdims=True))
        gbuf[l, 3 * per, 1:2, 0:half] = to_row(jnp.sum(dy_own, axis=1, keepdims=True))

    reducing = {}
    for l in range(layers - 1, -1, -1):
        dy_own = dy[l, own].astype(F32)
        if l > 0:
            if l < layers - 1:
                dh[...] = mm(wmix[l], dy[l])
            d_pre = dh[...] * pre_s[l]
            d_round = d_pre.astype(BF16)
            dr[...] = d_round
            dh[...] = d_pre
            share = (mm(wback[l, own_msg], d_round) * inverse).astype(BF16)
            incoming = []
            for step in range(1, reach + 1):
                for sign in (1, -1):
                    slot = reach + sign * step
                    part_out[l - 1, slot] = mm(share, adj[slot]).astype(BF16)
                    landing = reach - sign * step
                    incoming.append(
                        (
                            landing,
                            send(
                                part_out.at[l - 1, slot],
                                part_in.at[l - 1, landing],
                                s_ps.at[l - 1, landing],
                                s_pr.at[l - 1, landing],
                                {"blk": at(sign * step)},
                            ),
                        )
                    )
            before = dy_own + mm(wback[l, own], d_round) + share.astype(F32) + mm(share, adj[reach])
            if l == layers - 1:
                last = xm[l, own].astype(F32) + mm(wmixt[l, own], hid[l]) + ob[l][0]
                out_x[...] = last.astype(BF16)
            gradients(l, dh[own], dr[own], dy_own)
            reducing[l] = reduce_start(l)
            for landing, copy in incoming:
                copy.wait_recv()
                before = before + part_in[l - 1, landing].astype(F32)
            dy[l - 1, own] = before.astype(BF16)
            copy = to_peer(6 + layers + l, dy.at[l - 1, own], dy.at[l - 1, own])
            copy.wait_recv()
        else:
            d_own = mm(wmix[l, own], dy[l]) * pre_s[l, own]
            gradients(l, d_own, d_own.astype(BF16), dy_own)
            reducing[l] = reduce_start(l)
    sharing = {}
    for l in range(layers - 1, -1, -1):
        sharing[l] = reduce_end(l, reducing[l])
    for l in range(layers - 1, -1, -1):
        for copy in sharing[l]:
            copy.wait_recv()
    for copy in pending:
        copy.wait_send()


def finish(x_in, gred, w_node, w_msg, w_mix, a_node, a_msg, a_mix, out_x, g_node, g_msg, g_mix, g_hb, g_ob,
           wv, o_node, o_msg, o_mix, o_hb, o_ob, s_in, s_out):
    layers, half, feat = w_node.shape
    chunk = gred.shape[2]
    per = half // chunk
    loads = [
        pltpu.make_async_copy(src, wv.at[i], s_in.at[i])
        for i, src in enumerate((w_node, a_node, w_msg, a_msg, w_mix, a_mix))
    ]
    for copy in loads:
        copy.start()
    stores = [pltpu.make_async_copy(x_in, out_x, s_out.at[0])]
    stores[0].start()

    def leave(src, dst):
        copy = pltpu.make_async_copy(src, dst, s_out.at[len(stores)])
        copy.start()
        stores.append(copy)

    for l in range(layers):
        o_hb[l : l + 1] = gred[l, 3 * per, 0:1, 0:half]
        o_ob[l : l + 1] = gred[l, 3 * per, 1:2, 0:half]
    leave(o_hb, g_hb)
    leave(o_ob, g_ob)
    for i, (held, dst) in enumerate(((o_node, g_node), (o_msg, g_msg), (o_mix, g_mix))):
        loads[2 * i].wait()
        loads[2 * i + 1].wait()
        for l in range(layers):
            total = gred[l, i * per : (i + 1) * per].reshape(half, feat)
            held[l] = total + (wv[2 * i, l].astype(F32) - wv[2 * i + 1, l].astype(F32))
        leave(held, dst)
    for copy in stores:
        copy.wait()


def local(
    features, w_node, w_msg, w_mix, hbias, obias, anchor_node, anchor_msg, anchor_mix, cotangent,
    tile_cols, tile_count, tile_masks,
):
    br, slots, tile, _ = tile_masks.shape
    half, nodes = features.shape
    feat = 2 * half
    layers = w_node.shape[0]
    n = lax.axis_size("blk")
    reach = max(1, n // 8)
    wins = 2 * reach + 1
    chunk = max(8, 256 // n)
    dma = pltpu.SemaphoreType.DMA
    vmem = pl.BlockSpec(memory_space=pltpu.VMEM)
    hbm = pl.BlockSpec(memory_space=pltpu.HBM)
    w_node, w_msg, anchor_node, anchor_msg = (
        jnp.swapaxes(value, 1, 2) for value in (w_node, w_msg, anchor_node, anchor_msg)
    )
    last, sums = pl.pallas_call(
        functools.partial(kernel, n, reach, layers, br, slots, tile, half, nodes),
        out_shape=(
            jax.ShapeDtypeStruct((half, nodes), BF16),
            jax.ShapeDtypeStruct((layers, n, chunk, feat), F32),
        ),
        in_specs=[hbm] * 10,
        out_specs=(vmem,) * 2,
        scratch_shapes=[
            pltpu.SMEM((br, slots), jnp.int32),
            pltpu.SMEM((br,), jnp.int32),
            pltpu.VMEM((layers, half), F32),
            pltpu.VMEM((layers, half), F32),
            pltpu.VMEM((br, slots, tile, tile), jnp.int32),
            pltpu.VMEM((slots, tile, tile), BF16),
            pltpu.VMEM((wins, nodes, nodes), BF16),
            pltpu.VMEM((layers, wins, half, nodes), BF16),
            pltpu.VMEM((layers, 2 * feat, nodes), BF16),
            pltpu.VMEM((layers, feat, 2 * feat), BF16),
            pltpu.VMEM((layers, feat, feat), BF16),
            pltpu.VMEM((layers, feat, feat), BF16),
            pltpu.VMEM((layers, 2 * feat, feat), BF16),
            pltpu.VMEM((2, 8, 128), F32),
            pltpu.VMEM((layers, feat, nodes), BF16),
            pltpu.VMEM((layers, feat, nodes), F32),
            pltpu.VMEM((layers, feat, nodes), BF16),
            pltpu.VMEM((feat, nodes), BF16),
            pltpu.VMEM((feat, nodes), F32),
            pltpu.VMEM((layers - 1, wins, half, nodes), BF16),
            pltpu.VMEM((layers - 1, wins, half, nodes), BF16),
            pltpu.VMEM((layers, n, chunk, feat), F32),
            pltpu.VMEM((layers, n - 1, chunk, feat), F32),
            dma((10,)),
            dma((br,)),
            dma((layers, wins)),
            dma((layers, wins)),
            dma((layers - 1, wins)),
            dma((layers - 1, wins)),
            dma((6 + 2 * layers,)),
            dma((6 + 2 * layers,)),
            dma((layers, n - 1)),
            dma((layers, n - 1)),
            dma((layers, n - 1)),
            dma((layers, n - 1)),
        ],
        compiler_params=pltpu.CompilerParams(
            collective_id=0, has_side_effects=True, vmem_limit_bytes=56 * 1024 * 1024
        ),
        name="graph_net",
    )(tile_cols, tile_count, features, w_node, w_msg, w_mix, hbias, obias, cotangent, tile_masks)
    square = (layers, half, feat)
    out, g_node, g_msg, g_mix, g_hb, g_ob = pl.pallas_call(
        finish,
        out_shape=(
            jax.ShapeDtypeStruct((half, nodes), BF16),
            jax.ShapeDtypeStruct(square, F32),
            jax.ShapeDtypeStruct(square, F32),
            jax.ShapeDtypeStruct(square, F32),
            jax.ShapeDtypeStruct((layers, half), F32),
            jax.ShapeDtypeStruct((layers, half), F32),
        ),
        in_specs=[vmem] * 2 + [hbm] * 6,
        out_specs=(hbm,) * 6,
        scratch_shapes=[
            pltpu.VMEM((6,) + square, BF16),
            pltpu.VMEM(square, F32),
            pltpu.VMEM(square, F32),
            pltpu.VMEM(square, F32),
            pltpu.VMEM((layers, half), F32),
            pltpu.VMEM((layers, half), F32),
            dma((6,)),
            dma((6,)),
        ],
        name="finish",
    )(last, sums, w_node, w_msg, w_mix, anchor_node, anchor_msg, anchor_mix)
    return out, jnp.swapaxes(g_node, 1, 2), jnp.swapaxes(g_msg, 1, 2), g_mix, g_hb, g_ob


def solution(mesh):
    placed = (
        P(("member", "feat"), "blk"),
        P("member", None, "feat"),
        P("member", None, "feat"),
        P("member", "feat", None),
        P("member", "feat"),
        P("member", "feat"),
        P("member", None, "feat"),
        P("member", None, "feat"),
        P("member", "feat", None),
        P(("member", "feat"), "blk"),
        P(("member", "blk"), None),
        P(("member", "blk")),
        P(("member", "blk"), None, None, None),
    )
    return jax.shard_map(
        local,
        mesh=mesh,
        in_specs=placed,
        out_specs=(
            P(("member", "feat"), "blk"),
            P("member", None, "feat"),
            P("member", None, "feat"),
            P("member", "feat", None),
            P("member", "feat"),
            P("member", "feat"),
        ),
        check_vma=False,
    )
```

```python
import functools

import jax
import jax.numpy as jnp
from jax import lax
from jax.experimental import pallas as pl
from jax.experimental.pallas import tpu as pltpu
from jax.sharding import PartitionSpec as P

F32 = jnp.float32
BF16 = jnp.bfloat16
MESH = pl.DeviceIdType.MESH


def mm(left, right):
    return jnp.dot(left, right, preferred_element_type=F32)


def mm_nt(left, right):
    return lax.dot_general(left, right, (((1,), (1,)), ((), ())), preferred_element_type=F32)


def eye(size):
    rows = lax.broadcasted_iota(jnp.int32, (size, size), 0)
    cols = lax.broadcasted_iota(jnp.int32, (size, size), 1)
    return rows == cols


def to_column(row):
    size = row.shape[1]
    return jnp.sum(jnp.where(eye(size), jnp.broadcast_to(row, (size, size)), 0.0), axis=1, keepdims=True)


def to_row(column):
    size = column.shape[0]
    return jnp.sum(jnp.where(eye(size), jnp.broadcast_to(column, (size, size)), 0.0), axis=0, keepdims=True)


def kernel(
    n, reach, layers, br, slots, tile, half, nodes,
    cols, count, feats, w_node, w_msg, w_mix, hbias, obias, cot, masks,
    out_x, gred,
    cols_s, count_s, hb_v, ob_v, mask_v, mask_b, adj, xwin, xm, wt, wmix, wmixt, wback, bias, dy, pre_s, hid, dr, dh, part_out, part_in,
    gbuf, grecv, bias_s,
    s_in, s_mask, s_xs, s_xr, s_ps, s_pr, s_fs, s_fr, s_gs, s_gr, s_as, s_ar,
):
    feat = 2 * half
    me = lax.axis_index("blk")
    side = lax.axis_index("feat")
    peer = 1 - side
    wins = 2 * reach + 1
    own = pl.ds(pl.multiple_of(side * half, half), half)
    own_msg = pl.ds(pl.multiple_of(feat + side * half, half), half)
    far = pl.ds(pl.multiple_of(peer * half, half), half)
    chunk = gbuf.shape[2]

    def at(step):
        return lax.rem(me + step + n, n)

    barrier = pltpu.get_barrier_semaphore()
    pl.semaphore_signal(barrier, inc=1, device_id={"feat": peer}, device_id_type=MESH)
    for step in range(1, n):
        pl.semaphore_signal(barrier, inc=1, device_id={"blk": at(step)}, device_id_type=MESH)

    moves = [
        (cols, cols_s),
        (count, count_s),
        (hbias, hb_v),
        (obias, ob_v),
        (feats, xm.at[0, own]),
        (feats, xwin.at[0, reach]),
        (cot, dy.at[layers - 1, own]),
        (w_node, wt.at[:, own, 0:feat]),
        (w_msg, wt.at[:, own, feat : 2 * feat]),
        (w_mix, wmix.at[:, own]),
    ]
    loads = [pltpu.make_async_copy(src, dst, s_in.at[i]) for i, (src, dst) in enumerate(moves)]
    for copy in loads[0:4]:
        copy.start()
    mask_copies = [pltpu.make_async_copy(masks.at[r], mask_v.at[r], s_mask.at[r]) for r in range(br)]
    for copy in loads[4:] + mask_copies:
        copy.start()
    for copy in loads[0:4]:
        copy.wait()
    bias[side] = jnp.zeros(bias.shape[1:], F32)
    bias[side, 0:layers, 0:half] = hb_v[...]
    bias[side, layers : 2 * layers, 0:half] = ob_v[...]

    pl.semaphore_wait(barrier, n)

    pending = []

    def send(src, dst, s_send, s_recv, device):
        copy = pltpu.make_async_remote_copy(
            src_ref=src, dst_ref=dst, send_sem=s_send, recv_sem=s_recv, device_id=device, device_id_type=MESH
        )
        copy.start()
        pending.append(copy)
        return copy

    def spread_out(src, l):
        copies = []
        for step in range(1, reach + 1):
            for sign in (1, -1):
                slot = reach - sign * step
                copies.append(
                    (slot, send(src, xwin.at[l, slot], s_xs.at[l, slot], s_xr.at[l, slot], {"blk": at(sign * step)}))
                )
        return copies

    def to_peer(index, src, dst):
        return send(src, dst, s_fs.at[index], s_fr.at[index], {"feat": peer})

    arriving = spread_out(feats, 0)
    first = [
        to_peer(0, w_mix, wmix.at[:, own]),
        to_peer(1, w_node, wt.at[:, own, 0:feat]),
        to_peer(2, w_msg, wt.at[:, own, feat : 2 * feat]),
        to_peer(3, bias.at[side], bias.at[side]),
        to_peer(4, cot, dy.at[layers - 1, own]),
        to_peer(5, feats, xm.at[0, own]),
    ]

    for r in range(br):
        mask_copies[r].wait()

    def build_row(r, unused):
        for k in range(slots):
            mask_b[k] = mask_v[r, k].astype(F32).astype(BF16)
        live = count_s[r]
        targets = []
        for k in range(slots):
            name = cols_s[r, k]
            block = lax.rem(lax.div(name, br) - me + reach + n, n) * br + lax.rem(name, br)
            targets.append(jnp.where(k < live, block, -1))

        def build_dev(j, unused):
            rows = pl.ds(pl.multiple_of(r * tile, tile), tile)
            for c in range(br):
                total = jnp.zeros((tile, tile), BF16)
                for k in range(slots):
                    hit = jnp.where(targets[k] == j * br + c, 1.0, 0.0).astype(F32)
                    total = total + jnp.full((tile, tile), hit, F32).astype(BF16) * mask_b[k]
                adj[j, rows, c * tile : (c + 1) * tile] = total
            return unused

        return lax.fori_loop(0, wins, build_dev, unused)

    lax.fori_loop(0, br, build_row, 0)
    ones = jnp.ones((16, nodes), BF16)
    degree = mm_nt(ones, adj[0])
    for j in range(1, wins):
        degree = degree + mm_nt(ones, adj[j])
    inverse = 1.0 / (degree[0:1] + 1.0)

    for copy in loads[4:]:
        copy.wait()
    for copy in first[0:5]:
        copy.wait_recv()
    unit_f = jnp.where(eye(feat), 1.0, 0.0).astype(BF16)
    hb, ob = [], []
    for l in range(layers):
        wmixt[l] = mm_nt(unit_f, wmix[l]).astype(BF16)
        if l > 0:
            wback[l, 0:feat] = mm_nt(unit_f, wt[l, :, 0:feat]).astype(BF16)
            wback[l, feat : 2 * feat] = mm_nt(unit_f, wt[l, :, feat : 2 * feat]).astype(BF16)
        hb.append(
            jnp.concatenate([to_column(bias[s, l : l + 1, 0:half]) for s in range(2)], axis=0)
        )
        ob.append([to_column(bias[s, layers + l : layers + l + 1, 0:half]) for s in (side, peer)])
    dh[...] = mm(wmix[layers - 1], dy[layers - 1])
    first[5].wait_recv()

    for l in range(layers):
        summed = mm_nt(xwin[l, reach], adj[reach])
        for slot, copy in arriving:
            copy.wait_recv()
            summed = summed + mm_nt(xwin[l, slot], adj[slot])
        message = (xm[l, own].astype(F32) + summed) * inverse
        xm[l, own_msg] = message.astype(BF16)
        copy = to_peer(6 + l, xm.at[l, own_msg], xm.at[l, own_msg])
        part = mm(wt[l, :, 0:feat], xm[l, 0:feat]) + hb[l]
        copy.wait_recv()
        pre = part + mm(wt[l, :, feat : 2 * feat], xm[l, feat : 2 * feat])
        sigma = 1.0 / (1.0 + jnp.exp(-pre))
        hidden = (pre * sigma).astype(BF16)
        hid[l] = hidden
        slope = sigma * (1.0 + pre * (1.0 - sigma))
        pre_s[l] = slope
        if l + 1 < layers:
            after = (xm[l, own].astype(F32) + mm(wmixt[l, own], hidden) + ob[l][0]).astype(BF16)
            xm[l + 1, own] = after
            xwin[l + 1, reach] = after
            arriving = spread_out(xwin.at[l + 1, reach], l + 1)
            xm[l + 1, far] = (xm[l, far].astype(F32) + mm(wmixt[l, far], hidden) + ob[l][1]).astype(BF16)

    def reduce_start(l):
        copies = []
        for step in range(1, n):
            to = at(step)
            copies.append(
                send(gbuf.at[l, to], grecv.at[l, step - 1], s_gs.at[l, step - 1], s_gr.at[l, step - 1], {"blk": to})
            )
        return copies

    def reduce_end(l, copies):
        total = gbuf[l, me].astype(F32)
        for step in range(1, n):
            copies[step - 1].wait_recv()
            total = total + grecv[l, step - 1].astype(F32)
        low = jnp.concatenate([total[2:4], jnp.zeros((chunk - 2, feat), F32)], axis=0)
        row = lax.broadcasted_iota(jnp.int32, (chunk, feat), 0)
        pair = total + low
        high = pair.astype(BF16).astype(F32)
        rest = jnp.concatenate([jnp.zeros((2, feat), F32), (pair - high)[0 : chunk - 2]], axis=0)
        split = jnp.where(row < 2, high, rest)
        slot = lax.broadcasted_iota(jnp.int32, (chunk, feat), 0) * 0 + me
        gred[l, me] = jnp.where(slot == 3 * (half // chunk), split, total).astype(BF16)
        return [
            send(gred.at[l, me], gred.at[l, me], s_as.at[l, step - 1], s_ar.at[l, step - 1], {"blk": at(step)})
            for step in range(1, n)
        ]

    def gradients(l, d_own, d_round_own, dy_own):
        per = half // chunk
        gbuf[l, 0:per] = mm_nt(d_round_own, xm[l, 0:feat]).reshape(per, chunk, feat).astype(BF16)
        gbuf[l, per : 2 * per] = (
            mm_nt(d_round_own, xm[l, feat : 2 * feat]).reshape(per, chunk, feat).astype(BF16)
        )
        gbuf[l, 2 * per : 3 * per] = mm_nt(hid[l, own], dy[l]).reshape(per, chunk, feat).astype(BF16)
        if n > 3 * per + 1:
            gbuf[l, 3 * per + 1 :] = jnp.zeros((n - 3 * per - 1, chunk, feat), BF16)
        sums = jnp.concatenate(
            [
                to_row(jnp.sum(d_own, axis=1, keepdims=True)),
                to_row(jnp.sum(dy_own, axis=1, keepdims=True)),
            ],
            axis=0,
        )
        high = sums.astype(BF16).astype(F32)
        bias_s[...] = jnp.zeros(bias_s.shape, F32)
        bias_s[0:2, 0:half] = high
        bias_s[2:4, 0:half] = sums - high
        gbuf[l, 3 * per] = bias_s[...].astype(BF16)

    reducing = {}
    for l in range(layers - 1, -1, -1):
        dy_own = dy[l, own].astype(F32)
        if l > 0:
            if l < layers - 1:
                dh[...] = mm(wmix[l], dy[l])
            d_pre = dh[...] * pre_s[l]
            d_round = d_pre.astype(BF16)
            dr[...] = d_round
            dh[...] = d_pre
            share = (mm(wback[l, own_msg], d_round) * inverse).astype(BF16)
            incoming = []
            for step in range(1, reach + 1):
                for sign in (1, -1):
                    slot = reach + sign * step
                    part_out[l - 1, slot] = mm(share, adj[slot]).astype(BF16)
                    landing = reach - sign * step
                    incoming.append(
                        (
                            landing,
                            send(
                                part_out.at[l - 1, slot],
                                part_in.at[l - 1, landing],
                                s_ps.at[l - 1, landing],
                                s_pr.at[l - 1, landing],
                                {"blk": at(sign * step)},
                            ),
                        )
                    )
            before = dy_own + mm(wback[l, own], d_round) + share.astype(F32) + mm(share, adj[reach])
            if l == layers - 1:
                last = xm[l, own].astype(F32) + mm(wmixt[l, own], hid[l]) + ob[l][0]
                out_x[...] = last.astype(BF16)
            gradients(l, dh[own], dr[own], dy_own)
            for landing, copy in incoming:
                copy.wait_recv()
                before = before + part_in[l - 1, landing].astype(F32)
            dy[l - 1, own] = before.astype(BF16)
            copy = to_peer(6 + layers + l, dy.at[l - 1, own], dy.at[l - 1, own])
            reducing[l] = reduce_start(l)
            copy.wait_recv()
        else:
            d_own = mm(wmix[l, own], dy[l]) * pre_s[l, own]
            gradients(l, d_own, d_own.astype(BF16), dy_own)
            reducing[l] = reduce_start(l)
    sharing = {}
    for l in range(layers - 1, -1, -1):
        sharing[l] = reduce_end(l, reducing[l])
    for l in range(layers - 1, -1, -1):
        for copy in sharing[l]:
            copy.wait_recv()
    for copy in pending:
        copy.wait_send()


def finish(x_in, gred, w_node, w_msg, w_mix, a_node, a_msg, a_mix, out_x, g_node, g_msg, g_mix, g_hb, g_ob,
           wv, o_node, o_msg, o_mix, o_hb, o_ob, s_in, s_out):
    layers, half, feat = w_node.shape
    chunk = gred.shape[2]
    per = half // chunk
    loads = [
        pltpu.make_async_copy(src, wv.at[i], s_in.at[i])
        for i, src in enumerate((w_node, a_node, w_msg, a_msg, w_mix, a_mix))
    ]
    for copy in loads:
        copy.start()
    stores = [pltpu.make_async_copy(x_in, out_x, s_out.at[0])]
    stores[0].start()

    def leave(src, dst):
        copy = pltpu.make_async_copy(src, dst, s_out.at[len(stores)])
        copy.start()
        stores.append(copy)

    for l in range(layers):
        pair = gred[l, 3 * per].astype(F32)
        o_hb[l : l + 1] = pair[0:1, 0:half] + pair[2:3, 0:half]
        o_ob[l : l + 1] = pair[1:2, 0:half] + pair[3:4, 0:half]
    leave(o_hb, g_hb)
    leave(o_ob, g_ob)
    for i, (held, dst) in enumerate(((o_node, g_node), (o_msg, g_msg), (o_mix, g_mix))):
        loads[2 * i].wait()
        loads[2 * i + 1].wait()
        for l in range(layers):
            total = gred[l, i * per : (i + 1) * per].astype(F32).reshape(half, feat)
            held[l] = total + (wv[2 * i, l].astype(F32) - wv[2 * i + 1, l].astype(F32))
        leave(held, dst)
    for copy in stores:
        copy.wait()


def local(
    features, w_node, w_msg, w_mix, hbias, obias, anchor_node, anchor_msg, anchor_mix, cotangent,
    tile_cols, tile_count, tile_masks,
):
    br, slots, tile, _ = tile_masks.shape
    half, nodes = features.shape
    feat = 2 * half
    layers = w_node.shape[0]
    n = lax.axis_size("blk")
    reach = max(1, n // 8)
    wins = 2 * reach + 1
    chunk = max(16, 256 // n)
    dma = pltpu.SemaphoreType.DMA
    vmem = pl.BlockSpec(memory_space=pltpu.VMEM)
    hbm = pl.BlockSpec(memory_space=pltpu.HBM)
    w_node, w_msg, anchor_node, anchor_msg = (
        jnp.swapaxes(value, 1, 2) for value in (w_node, w_msg, anchor_node, anchor_msg)
    )
    last, sums = pl.pallas_call(
        functools.partial(kernel, n, reach, layers, br, slots, tile, half, nodes),
        out_shape=(
            jax.ShapeDtypeStruct((half, nodes), BF16),
            jax.ShapeDtypeStruct((layers, n, chunk, feat), BF16),
        ),
        in_specs=[hbm] * 10,
        out_specs=(vmem,) * 2,
        scratch_shapes=[
            pltpu.SMEM((br, slots), jnp.int32),
            pltpu.SMEM((br,), jnp.int32),
            pltpu.VMEM((layers, half), F32),
            pltpu.VMEM((layers, half), F32),
            pltpu.VMEM((br, slots, tile, tile), jnp.int32),
            pltpu.VMEM((slots, tile, tile), BF16),
            pltpu.VMEM((wins, nodes, nodes), BF16),
            pltpu.VMEM((layers, wins, half, nodes), BF16),
            pltpu.VMEM((layers, 2 * feat, nodes), BF16),
            pltpu.VMEM((layers, feat, 2 * feat), BF16),
            pltpu.VMEM((layers, feat, feat), BF16),
            pltpu.VMEM((layers, feat, feat), BF16),
            pltpu.VMEM((layers, 2 * feat, feat), BF16),
            pltpu.VMEM((2, 8, 128), F32),
            pltpu.VMEM((layers, feat, nodes), BF16),
            pltpu.VMEM((layers, feat, nodes), F32),
            pltpu.VMEM((layers, feat, nodes), BF16),
            pltpu.VMEM((feat, nodes), BF16),
            pltpu.VMEM((feat, nodes), F32),
            pltpu.VMEM((layers - 1, wins, half, nodes), BF16),
            pltpu.VMEM((layers - 1, wins, half, nodes), BF16),
            pltpu.VMEM((layers, n, chunk, feat), BF16),
            pltpu.VMEM((layers, n - 1, chunk, feat), BF16),
            pltpu.VMEM((chunk, feat), F32),
            dma((10,)),
            dma((br,)),
            dma((layers, wins)),
            dma((layers, wins)),
            dma((layers - 1, wins)),
            dma((layers - 1, wins)),
            dma((6 + 2 * layers,)),
            dma((6 + 2 * layers,)),
            dma((layers, n - 1)),
            dma((layers, n - 1)),
            dma((layers, n - 1)),
            dma((layers, n - 1)),
        ],
        compiler_params=pltpu.CompilerParams(
            collective_id=0, has_side_effects=True, vmem_limit_bytes=56 * 1024 * 1024
        ),
        name="graph_net",
    )(tile_cols, tile_count, features, w_node, w_msg, w_mix, hbias, obias, cotangent, tile_masks)
    square = (layers, half, feat)
    out, g_node, g_msg, g_mix, g_hb, g_ob = pl.pallas_call(
        finish,
        out_shape=(
            jax.ShapeDtypeStruct((half, nodes), BF16),
            jax.ShapeDtypeStruct(square, F32),
            jax.ShapeDtypeStruct(square, F32),
            jax.ShapeDtypeStruct(square, F32),
            jax.ShapeDtypeStruct((layers, half), F32),
            jax.ShapeDtypeStruct((layers, half), F32),
        ),
        in_specs=[vmem] * 2 + [hbm] * 6,
        out_specs=(hbm,) * 6,
        scratch_shapes=[
            pltpu.VMEM((6,) + square, BF16),
            pltpu.VMEM(square, F32),
            pltpu.VMEM(square, F32),
            pltpu.VMEM(square, F32),
            pltpu.VMEM((layers, half), F32),
            pltpu.VMEM((layers, half), F32),
            dma((6,)),
            dma((6,)),
        ],
        name="finish",
    )(last, sums, w_node, w_msg, w_mix, anchor_node, anchor_msg, anchor_mix)
    return out, jnp.swapaxes(g_node, 1, 2), jnp.swapaxes(g_msg, 1, 2), g_mix, g_hb, g_ob


def solution(mesh):
    placed = (
        P(("member", "feat"), "blk"),
        P("member", None, "feat"),
        P("member", None, "feat"),
        P("member", "feat", None),
        P("member", "feat"),
        P("member", "feat"),
        P("member", None, "feat"),
        P("member", None, "feat"),
        P("member", "feat", None),
        P(("member", "feat"), "blk"),
        P(("member", "blk"), None),
        P(("member", "blk")),
        P(("member", "blk"), None, None, None),
    )
    return jax.shard_map(
        local,
        mesh=mesh,
        in_specs=placed,
        out_specs=(
            P(("member", "feat"), "blk"),
            P("member", None, "feat"),
            P("member", None, "feat"),
            P("member", "feat", None),
            P("member", "feat"),
            P("member", "feat"),
        ),
        check_vma=False,
    )
```
